32 devices in a mesh: sec: 16 (over z, y, core), rad: 2 (over x).
Axes of the slice: x: 2, y: 2, z: 4, core: 2. Of those that a mesh axis runs over, the one named last changes fastest.
Arguments:
- transmembrane_potential: float32 [4096, 256], P(('sec', 'rad')), may hold values from -0.8 to -0.3
- channel_openness: float32 [3, 4096, 256], P(None, ('sec', 'rad')), may hold values from 0.02 to 0.95
- longitudinal_conductance: float32 [4096], P(('sec', 'rad')), may hold values from 0.05 to 0.4
- sector_map: int32 [4096, 1], P(('sec', 'rad')), may hold values from 0 to 15; in each aligned block of 128 rows (0 to 127, 128 to 255, ...) at most 16 rows name the same one
- cell_index: int32 [4096], P(('sec', 'rad')), may hold values from 0 to 4095
- innervating_neuron: int32 [4096], P(('sec', 'rad')), may hold values from 0 to 511
- activation_moment: int32 [512], replicated, may hold values from 0 to 19
- synapse_position: int32 [4096], P(('sec', 'rad')), may hold values from 64 to 191
- radial_basis_matrix: float32 [256, 256], replicated, may hold values from -0.375 to 0.375
- spectrum: float32 [256, 512], P('sec'), may hold values from 1 to 20
Outputs:
- transmembrane_potential_later: float32 [4096, 256], P(('sec', 'rad'))
- channel_openness_later: float32 [3, 4096, 256], P(None, ('sec', 'rad'))
- potential: float32 [256, 256, 2, 512], P('sec', 'rad')
The draws below stay inside these ranges and needn't reach their ends.
Inputs may be any that keep to these rules, and one draw needn't show every extreme that they name: `sector_map`: among the 128 fibres of one device, at most 16 lie in any one sector.
All inputs are finite; a program needn't handle non-finite values.
Results may differ from the reference program's by a relative error of at most 0.00007.
Values sent between devices are 32-bit elements; how exact they have to be, the bound alone decides.
No kernel may reach another device: no remote copies, remote signals or barrier semaphores. Data moves between devices by JAX's collectives and lax.ppermute only.
A program may use at most 64 MiB of HBM per device.

```python
import math
import jax
import jax.numpy as jnp
import numpy as np
from jax import lax

AZ = 512
RAD = 256
AXIAL = 256
FIB_DEV = 128
MUS = 512
SUBSTEPS = 10
CAP = 16
CELLS = 4096
FIBRES = 4096
N_SEC = 16
N_RAD = 2


def touch_ends(array, own_key, least, high):
    index_at = [jax.random.randint(jax.random.fold_in(own_key, axis), (), 0, length) for axis, length in enumerate(array.shape)]
    widest = array.shape.index(max(array.shape))
    next_to = index_at[:widest] + [(index_at[widest] + 1) % array.shape[widest]] + index_at[widest + 1:]
    return array.at[tuple(index_at)].set(least).at[tuple(next_to)].set(high)


def level_of(key, shape, shards, low, largest):
    loudness, own = 1.0, jax.random.fold_in(key, 6)
    for axis_at, parts in shards:
        heights = jnp.exp(jax.random.uniform(jax.random.fold_in(own, axis_at), (parts,), jnp.float32, low / len(shards), largest / len(shards)))
        loudness = loudness * jnp.repeat(heights, shape[axis_at] // parts).reshape([-1 if axis == axis_at else 1 for axis in range(len(shape))])
    return loudness


def rank_bounds(count, skew):
    weights = [(1 << 20) // math.isqrt(standing ** skew) + 1 for standing in range(1, count + 1)]
    scale = 1 + sum(weights) // (1 << 30)
    return np.cumsum(np.array([max(1, weight // scale) for weight in weights]))


def ranked(stream_key, shape, count, slope):
    grid = rank_bounds(count, slope)
    lot = jax.random.randint(jax.random.fold_in(stream_key, 1), shape, 0, int(grid[count - 1]))
    standing = jnp.searchsorted(jnp.asarray(grid, jnp.int32), lot, side="right")
    return jax.random.permutation(jax.random.fold_in(stream_key, 2), count)[standing].astype(jnp.int32)


def shared_out(own_key, own, number, rows, amount, top, most, lean):
    sequence = jax.random.permutation(own_key, amount)
    crowded, usual = portions_of(amount, rows * top, most, lean, True), portions_of(amount, rows * top, most, lean, False)
    places = jnp.arange(amount)

    def named(lengths, rotation):
        used = int((lengths > 0).sum())
        fixed = max(1, used // 4)
        passed = fixed + (places - fixed + rotation * (used - fixed)) % max(1, amount - fixed)
        return jnp.zeros((amount,), jnp.int32).at[sequence[jnp.where(places < fixed, places, passed)]].set(jnp.asarray(lengths, jnp.int32))

    lengths = jnp.where(number % 4 == 0, named(crowded, number // 4), named(usual, number - number // 4 - 1))
    mixed = jax.random.permutation(jax.random.fold_in(own, 3), amount)
    donor, sink = mixed[0:amount // 2 * 2:2], mixed[1:amount // 2 * 2:2]
    room = jnp.minimum(lengths[donor] - 1, most - lengths[sink]) // 2
    room = jnp.where((donor == sequence[0]) | (sink == sequence[0]) | (lengths[sink] == 0), 0, jnp.maximum(room, 0))
    passed = jax.random.randint(jax.random.fold_in(own, 4), (amount // 2,), 0, 1 << 20) % (room + 1)
    lengths = lengths.at[donor].add(-passed).at[sink].add(passed)
    items = jnp.searchsorted(jnp.cumsum(lengths), jnp.arange(rows * top), side="right").astype(jnp.int32)
    table = items.reshape(top, rows).T
    table = table[jax.random.permutation(jax.random.fold_in(own, 1), rows)]
    rotation = jax.random.randint(jax.random.fold_in(own, 2), (rows, 1), 0, top)
    return jnp.take_along_axis(table, (jnp.arange(top)[None, :] + rotation) % top, axis=1)


def portions_of(count, total, limit, lean, full):
    portions = [(1 << 20) // math.isqrt(grade ** lean) + 1 for grade in range(1, count + 1)]
    largest = limit if full else min(limit, max(-(-total // count), total * portions[0] // sum(portions)))
    least = 1 if total - largest >= count - 1 else 0
    given, surplus = [largest] + [least] * (count - 1), total - largest - least * (count - 1)
    while surplus > 0:
        free = [i for i in range(1, count) if given[i] < largest] or [i for i in range(1, count) if given[i] < limit]
        mass, remaining = sum([portions[i] for i in free]), surplus
        for i in free:
            addition = min(limit - given[i], max(1, remaining * portions[i] // mass), surplus)
            given[i] = given[i] + addition
            surplus = surplus - addition
    return np.array(given)


def gaussian(key, shape, deviation, limit, held_as=jnp.bfloat16):
    return jnp.clip(deviation * jax.random.normal(key, shape, jnp.float32), -limit, limit).astype(held_as)


def setup_inputs(seed: int = 0) -> dict:
    splits = jax.random.split(jax.random.key(seed), 11)
    transmembrane_potential = jnp.clip(-0.8 + 0.5 * jax.random.uniform(splits[0], (FIBRES, AXIAL), jnp.float32) ** level_of(splits[0], (FIBRES, AXIAL), ((0, 32),), -0.2, 0.2), -0.8, -0.3)
    channel_openness = jnp.clip(0.02 + 0.93 * jax.random.uniform(splits[1], (3, FIBRES, AXIAL), jnp.float32) ** level_of(splits[1], (3, FIBRES, AXIAL), ((1, 32),), -0.2, 0.2), 0.02, 0.95)
    longitudinal_conductance = jnp.clip(jnp.exp(math.log(0.4) - 2.0794415 * jax.random.uniform(splits[2], (FIBRES,), jnp.float32) ** level_of(splits[2], (FIBRES,), ((0, 32),), -0.2, 0.2)), 0.05, 0.4)
    sector_map_keys = jax.random.split(jax.random.fold_in(splits[3], 1), FIBRES // FIB_DEV)
    sector_map_turns = jax.random.permutation(jax.random.fold_in(splits[3], 3), FIBRES // FIB_DEV)
    sector_map = jax.vmap(lambda own, number: shared_out(jax.random.fold_in(splits[3], 2), own, number, FIB_DEV, N_SEC, 1, CAP, 2))(sector_map_keys, sector_map_turns).reshape((FIBRES, 1))
    cell_index = touch_ends(jax.random.randint(splits[4], (FIBRES,), 0, CELLS), jax.random.fold_in(splits[4], 1), 0, CELLS - 1).astype(jnp.int32)
    innervating_neuron = touch_ends(ranked(splits[5], (FIBRES,), MUS, 2), jax.random.fold_in(splits[5], 3), 0, MUS - 1).astype(jnp.int32)
    activation_moment = touch_ends(jax.random.randint(splits[6], (MUS,), 0, 2 * SUBSTEPS), jax.random.fold_in(splits[6], 1), 0, (2 * SUBSTEPS) - 1).astype(jnp.int32)
    synapse_position = touch_ends(jax.random.randint(splits[7], (FIBRES,), AXIAL // 4, 3 * AXIAL // 4), jax.random.fold_in(splits[7], 1), AXIAL // 4, (3 * AXIAL // 4) - 1).astype(jnp.int32)
    radial_basis_matrix = gaussian(splits[8], (RAD, RAD), RAD ** -0.5, 0.375, jnp.float32)
    spectrum = jnp.clip(jnp.exp(math.log(20.0) - 2.9957323 * jax.random.uniform(splits[9], (RAD, AZ), jnp.float32) ** level_of(splits[9], (RAD, AZ), ((0, 16),), -0.2, 0.2)), 1.0, 20.0)
    return {"transmembrane_potential": transmembrane_potential, "channel_openness": channel_openness, "longitudinal_conductance": longitudinal_conductance, "sector_map": sector_map, "cell_index": cell_index, "innervating_neuron": innervating_neuron, "activation_moment": activation_moment, "synapse_position": synapse_position, "radial_basis_matrix": radial_basis_matrix, "spectrum": spectrum}


TIME_STEP = 0.005
G_SODIUM = 120.0
G_POTASSIUM = 36.0
G_LEAK = 0.3
E_SODIUM = 50.0
E_POTASSIUM = -77.0
E_LEAK = -54.4
APPLIED_AMPERES = 800.0


def second_diff(values):
    left_side = jnp.concatenate([values[:, :1], values[:, :-1]], 1)
    right_side = jnp.concatenate([values[:, 1:], values[:, -1:]], 1)
    return left_side + right_side - 2.0 * values


def sarcolemma_model(transmembrane_potential, channel_openness, longitudinal_conductance, activation_substep_count, synapse_position):
    points = lax.broadcasted_iota(jnp.int32, transmembrane_potential.shape, 1)
    destination_position = (points == synapse_position[:, None]).astype(jnp.float32)

    def substep(present_substep_counter, state_pair):
        volt_now, gate_now = state_pair
        membrane_mv = 100.0 * volt_now
        ionic = (G_SODIUM * gate_now[0] ** 3 * gate_now[1] * (membrane_mv - E_SODIUM)
                 + G_POTASSIUM * gate_now[2] ** 4 * (membrane_mv - E_POTASSIUM)
                 + G_LEAK * (membrane_mv - E_LEAK))
        activation_markers = (present_substep_counter >= activation_substep_count)[:, None].astype(jnp.float32)
        applied_excitation = APPLIED_AMPERES * destination_position * activation_markers
        opening = jnp.stack([jax.nn.softplus((membrane_mv + 40.0) / 10.0),
                             0.07 * jnp.exp(-(membrane_mv + 65.0) / 20.0),
                             0.1 * jax.nn.softplus((membrane_mv + 55.0) / 10.0)])
        closing = jnp.stack([4.0 * jnp.exp(-(membrane_mv + 65.0) / 18.0),
                             jax.nn.sigmoid((membrane_mv + 35.0) / 10.0),
                             0.125 * jnp.exp(-(membrane_mv + 65.0) / 80.0)])
        rate_sum = opening + closing
        steady = opening / rate_sum
        gate_after = steady + (gate_now - steady) * jnp.exp(-TIME_STEP * rate_sum)
        volt_after = volt_now + longitudinal_conductance[:, None] * second_diff(volt_now) + (TIME_STEP / 100.0) * (applied_excitation - ionic)
        return volt_after, gate_after

    return lax.fori_loop(0, SUBSTEPS, substep, (transmembrane_potential, channel_openness))


def reference(transmembrane_potential, channel_openness, longitudinal_conductance, sector_map, cell_index, innervating_neuron, activation_moment, synapse_position, radial_basis_matrix, spectrum):
    activation_substep_count = activation_moment[innervating_neuron]
    transmembrane_potential_later, channel_openness_later = sarcolemma_model(transmembrane_potential, channel_openness, longitudinal_conductance, activation_substep_count, synapse_position)
    source = longitudinal_conductance[:, None] * second_diff(transmembrane_potential_later)
    sector_width = AZ // N_SEC
    band_rows = RAD // N_RAD
    fibre_index = jnp.arange(FIBRES, dtype=jnp.int32)
    band_index = (fibre_index // FIB_DEV) % N_RAD
    azimuth = sector_map[:, 0] * sector_width + cell_index // band_rows
    radius = band_index * band_rows + cell_index % band_rows
    source_grid = jnp.zeros((AZ, RAD, AXIAL), jnp.float32).at[azimuth, radius].add(source)
    projected = jnp.einsum("arx,rj->ajx", source_grid, radial_basis_matrix, precision=lax.Precision.HIGHEST)
    spectral = jnp.fft.fft(projected, axis=0, norm="ortho")
    mode_scale = spectrum[:, None, :]
    real_part = jnp.transpose(spectral.real, (1, 2, 0)) * mode_scale
    imag_part = jnp.transpose(spectral.imag, (1, 2, 0)) * mode_scale
    potential = jnp.stack([real_part, imag_part], 2).astype(jnp.float32)
    return transmembrane_potential_later, channel_openness_later, potential
```

```python
import math

import functools

import jax
import jax.numpy as jnp
import numpy as np
from jax import lax
from jax.experimental import pallas as pl
from jax.experimental.pallas import tpu as pltpu
from jax.sharding import PartitionSpec as P

AZ = 512
RAD = 256
SUBSTEPS = 10


TIME_STEP = 0.005
G_SODIUM = 120.0
G_POTASSIUM = 36.0
G_LEAK = 0.3
E_SODIUM = 50.0
E_POTASSIUM = -77.0
E_LEAK = -54.4
APPLIED_AMPERES = 800.0


def second_diff(values):
    left_side = jnp.concatenate([values[:, :1], values[:, :-1]], 1)
    right_side = jnp.concatenate([values[:, 1:], values[:, -1:]], 1)
    return left_side + right_side - 2.0 * values


def sarcolemma_model(
    transmembrane_potential,
    channel_openness,
    longitudinal_conductance,
    activation_substep_count,
    synapse_position,
):
    points = lax.broadcasted_iota(jnp.int32, transmembrane_potential.shape, 1)
    destination_position = (points == synapse_position[:, None]).astype(jnp.float32)

    def substep(present_substep_counter, state_pair):
        volt_now, gate_now = state_pair
        membrane_mv = 100.0 * volt_now
        ionic = (
            G_SODIUM * gate_now[0] ** 3 * gate_now[1] * (membrane_mv - E_SODIUM)
            + G_POTASSIUM * gate_now[2] ** 4 * (membrane_mv - E_POTASSIUM)
            + G_LEAK * (membrane_mv - E_LEAK)
        )
        activation_markers = (present_substep_counter >= activation_substep_count)[:, None].astype(
            jnp.float32
        )
        applied_excitation = APPLIED_AMPERES * destination_position * activation_markers
        opening = jnp.stack(
            [
                jax.nn.softplus((membrane_mv + 40.0) / 10.0),
                0.07 * jnp.exp(-(membrane_mv + 65.0) / 20.0),
                0.1 * jax.nn.softplus((membrane_mv + 55.0) / 10.0),
            ]
        )
        closing = jnp.stack(
            [
                4.0 * jnp.exp(-(membrane_mv + 65.0) / 18.0),
                jax.nn.sigmoid((membrane_mv + 35.0) / 10.0),
                0.125 * jnp.exp(-(membrane_mv + 65.0) / 80.0),
            ]
        )
        rate_sum = opening + closing
        steady = opening / rate_sum
        gate_after = steady + (gate_now - steady) * jnp.exp(-TIME_STEP * rate_sum)
        volt_after = (
            volt_now
            + longitudinal_conductance[:, None] * second_diff(volt_now)
            + TIME_STEP / 100.0 * (applied_excitation - ionic)
        )
        return (volt_after, gate_after)

    return lax.fori_loop(0, SUBSTEPS, substep, (transmembrane_potential, channel_openness))


def per_device_general(
    transmembrane_potential,
    channel_openness,
    longitudinal_conductance,
    sector_map,
    cell_index,
    innervating_neuron,
    activation_moment,
    synapse_position,
    radial_basis_matrix,
    spectrum,
):
    fibres, point_count = transmembrane_potential.shape
    unit_count = activation_moment.shape[0]
    unit_ids = lax.broadcasted_iota(jnp.int32, (fibres, unit_count), 1)
    activation_substep_count = jnp.sum(
        jnp.where(innervating_neuron[:, None] == unit_ids, activation_moment[None, :], 0), 1
    )
    transmembrane_potential_later, channel_openness_later = sarcolemma_model(
        transmembrane_potential,
        channel_openness,
        longitudinal_conductance,
        activation_substep_count,
        synapse_position,
    )
    source = longitudinal_conductance[:, None] * second_diff(transmembrane_potential_later)
    sectors = lax.axis_size("sec")
    band_count = lax.axis_size("rad")
    sector_width = AZ // sectors
    band_rows = RAD // band_count
    cell_count = sector_width * band_rows
    capacity = 2 * fibres // sectors
    slot_count = sectors * capacity
    chosen = sector_map[:, 0]
    member = (chosen[:, None] == lax.broadcasted_iota(jnp.int32, (fibres, sectors), 1)).astype(
        jnp.int32
    )
    slot_rank = jnp.sum(member * (jnp.cumsum(member, 0) - 1), 1)
    destination = chosen * capacity + slot_rank
    slot_ids = lax.broadcasted_iota(jnp.int32, (slot_count, fibres), 0)
    deposit_placement = (slot_ids == destination[None, :]).astype(jnp.float32)
    placed = jnp.dot(
        deposit_placement,
        source,
        precision=lax.Precision.HIGHEST,
        preferred_element_type=jnp.float32,
    )
    cell_code = cell_index % band_rows * sector_width + cell_index // band_rows + 1
    slot_codes = jnp.dot(
        deposit_placement,
        cell_code.astype(jnp.float32),
        precision=lax.Precision.HIGHEST,
        preferred_element_type=jnp.float32,
    )
    slab_width = point_count // band_count
    pieces = placed.reshape(slot_count, band_count, slab_width)
    spread_codes = jnp.broadcast_to(slot_codes[:, None], (slot_count, band_count))
    pieces, spread_codes = (
        lax.all_to_all(
            lax.all_to_all(pieces, "sec", split_axis=0, concat_axis=0, tiled=True),
            "rad",
            split_axis=1,
            concat_axis=1,
            tiled=True,
        ),
        lax.all_to_all(
            lax.all_to_all(spread_codes, "sec", split_axis=0, concat_axis=0, tiled=True),
            "rad",
            split_axis=1,
            concat_axis=1,
            tiled=True,
        ),
    )
    cell_ids = lax.broadcasted_iota(jnp.int32, (slot_count, band_count, cell_count), 2)
    onehot = (spread_codes.astype(jnp.int32)[:, :, None] - 1 == cell_ids).astype(jnp.float32)
    deposited = jnp.einsum("snx,snc->xnc", pieces, onehot, precision=lax.Precision.HIGHEST)
    radial_field = deposited.reshape(slab_width, RAD, sector_width)
    projected = jnp.einsum(
        "xra,rj->jxa", radial_field, radial_basis_matrix, precision=lax.Precision.HIGHEST
    )
    all_azimuths = lax.all_to_all(projected, "sec", split_axis=0, concat_axis=2, tiled=True)
    basis_local = all_azimuths.shape[0]
    slab_local = all_azimuths.shape[1]
    row_ids = lax.broadcasted_iota(jnp.int32, (AZ, AZ), 0)
    col_ids = lax.broadcasted_iota(jnp.int32, (AZ, AZ), 1)
    phase = (row_ids * col_ids % AZ).astype(jnp.float32) * (2.0 * math.pi / AZ)
    dft_table = jnp.concatenate([jnp.cos(phase), -jnp.sin(phase)], 1) * (1.0 / math.sqrt(AZ))
    flattened = all_azimuths.reshape(basis_local * slab_local, AZ)
    spectral = jnp.dot(
        flattened, dft_table, precision=lax.Precision.HIGHEST, preferred_element_type=jnp.float32
    )
    spectral = spectral.reshape(basis_local, slab_local, 2, AZ)
    potential = spectral * spectrum[:, None, None, :]
    return (transmembrane_potential_later, channel_openness_later, potential)


F32 = jnp.float32
BF16 = jnp.bfloat16


def iota(shape, axis):
    return lax.broadcasted_iota(jnp.int32, shape, axis).astype(F32)


def column(row, lanes):
    count = row.shape[1]
    wide = jnp.transpose(jnp.broadcast_to(row, (count, count)))
    return jnp.concatenate([wide] * (lanes // count), 1) if lanes > count else wide


def split(values):
    high = values.astype(BF16)
    return high, (values - high.astype(F32)).astype(BF16)


def fibre_kernel(
    band_ref,
    volt_ref,
    gate_ref,
    cond_ref,
    sector_ref,
    cell_ref,
    unit_ref,
    moment_ref,
    synapse_ref,
    volt_out,
    gate_out,
    pieces_out,
    fire_scratch,
    cond_scratch,
    *,
    sectors,
    sector_width,
    band_rows,
    chunk,
):
    fibres, points = volt_ref.shape
    bands, _, slab = pieces_out.shape
    units = moment_ref.shape[1]
    band = band_ref[0]
    chosen = (iota((units, fibres), 0) == unit_ref[...].astype(F32)).astype(BF16)
    moments = jnp.broadcast_to(moment_ref[...].astype(F32), (8, units)).astype(BF16)
    fire_row = jnp.dot(moments, chosen, preferred_element_type=F32)[:1]
    at_synapse = iota((fibres, points), 1) == column(synapse_ref[...].astype(F32), points)
    fire_scratch[...] = jnp.where(at_synapse, column(fire_row, points), 1e6)
    cond_scratch[...] = column(cond_ref[...], points)
    volt_out[...] = volt_ref[...]
    gate_out[...] = gate_ref[...]

    def curvature(values):
        where = lax.broadcasted_iota(jnp.int32, values.shape, 1)
        left = jnp.where(where == 0, values, pltpu.roll(values, 1, 1))
        right = jnp.where(where == points - 1, values, pltpu.roll(values, points - 1, 1))
        return left + right - 2.0 * values

    def substep(step, carry):
        now = step.astype(F32)
        for start in range(0, fibres, chunk):
            rows = pl.ds(start, chunk)
            volt = volt_out[rows, :]
            gate_m, gate_h, gate_n = gate_out[0, rows, :], gate_out[1, rows, :], gate_out[2, rows, :]
            mv = 100.0 * volt
            rest = mv + 65.0
            e80 = jnp.exp(rest * (-1.0 / 80.0))
            e40 = e80 * e80
            e20 = e40 * e40
            e10 = e20 * e20
            up = jnp.exp(rest * 0.1)
            alpha_m = jnp.log(1.0 + math.exp(-2.5) * up)
            alpha_h = 0.07 * e20
            alpha_n = 0.1 * jnp.log(1.0 + math.exp(-1.0) * up)
            beta_m = 4.0 * jnp.exp(rest * (-1.0 / 18.0))
            beta_h = 1.0 / (1.0 + math.exp(3.0) * e10)
            beta_n = 0.125 * e80
            square_n = gate_n * gate_n
            ionic = (
                G_SODIUM * (gate_m * gate_m * gate_m) * gate_h * (mv - E_SODIUM)
                + G_POTASSIUM * (square_n * square_n) * (mv - E_POTASSIUM)
                + G_LEAK * (mv - E_LEAK)
            )
            stimulus = jnp.where(now >= fire_scratch[rows, :], APPLIED_AMPERES, 0.0)
            for index, (gate, alpha, beta) in enumerate(
                ((gate_m, alpha_m, beta_m), (gate_h, alpha_h, beta_h), (gate_n, alpha_n, beta_n))
            ):
                rate = alpha + beta
                steady = alpha / rate
                gate_out[index, rows, :] = steady + (gate - steady) * jnp.exp(-TIME_STEP * rate)
            volt_out[rows, :] = (
                volt
                + cond_scratch[rows, :] * curvature(volt)
                + (TIME_STEP / 100.0) * (stimulus - ionic)
            )
        return carry

    lax.fori_loop(0, SUBSTEPS, substep, 0)
    source = cond_scratch[...] * curvature(volt_out[...])

    sector = sector_ref[...].astype(F32)
    earlier = (column(sector, fibres) == sector) & (iota((fibres, fibres), 0) < iota((fibres, fibres), 1))
    rank = jnp.sum(earlier.astype(F32), 0, keepdims=True)
    capacity = 2 * fibres // sectors
    slot = sector * capacity + rank
    cell = cell_ref[...]
    within = cell // band_rows
    half = sector_width // 2
    ordered = (within % 2) * half + within // 2
    radius = (cell % band_rows).astype(F32) + (band * band_rows).astype(F32)
    in_sector = (iota((sectors, fibres), 0) == sector).astype(F32)
    digits = jnp.concatenate(
        [in_sector * radius, in_sector * (ordered.astype(F32) + 1.0)], 0
    ).astype(BF16)
    in_rank = (column(rank, fibres) == iota((fibres, fibres), 1)).astype(BF16)
    table = jnp.dot(digits, in_rank, preferred_element_type=F32)
    table = table[:sectors] + (bands * band_rows) * table[sectors:]
    meta = table[:8]
    for group in range(1, sectors // 8):
        meta = meta + pltpu.roll(table[8 * group : 8 * group + 8], group * capacity, 1)
    slots = jnp.broadcast_to(slot, (8, fibres))
    lane, line = iota((8, fibres), 1), iota((8, fibres), 0)
    middle = fibres // 2
    meta = jnp.where((lane >= middle) & (line == 0), pltpu.roll(slots, middle, 1), meta)
    meta = jnp.where((lane >= middle) & (line == 1), slots, meta)
    for offset in range(bands):
        lanes = pl.ds(pl.multiple_of(((band + offset) % bands) * slab, slab), slab)
        fire_scratch[...] = source
        pieces_out[offset, :fibres, :] = fire_scratch[:, lanes]
        pieces_out[offset, fibres:, :] = meta


def grid_kernel(start_ref, *refs, count, sectors, sector_width, group):
    pieces = refs[:count]
    basis_ref, table_high, table_low, spectrum_ref, out_ref, placed, columns, basis_t, scales = refs[count:]
    fibres = pieces[0].shape[0] - 8
    slab = pieces[0].shape[1]
    capacity = 2 * fibres // sectors
    radii = basis_ref.shape[0]
    own = spectrum_ref.shape[0]
    slots = sectors * capacity
    depth = count * capacity
    half = sector_width // 2
    step = pl.program_id(0)

    @pl.when(step == 0)
    def _():
        basis_t[...] = jnp.transpose(basis_ref[...])
        for j in range(own):
            scales[j] = jnp.broadcast_to(spectrum_ref[j : j + 1, :], scales.shape[1:])
        mine = basis_t[pl.ds(pl.multiple_of(start_ref[0], 8), own), :]
        basis_pair = jnp.concatenate(split(mine), 0)
        lane8 = lax.broadcasted_iota(jnp.int32, (8, slab), 1)
        code_parts = [[jnp.zeros((8, slab), F32) for _ in range(depth // slab)] for _ in range(sectors // 8)]
        per = slab // capacity
        for d in range(count):
            values = pieces[d][:fibres, :]
            meta = pieces[d][fibres:, :]
            slot = jnp.where(lane8[:1] < fibres // 2, pltpu.roll(meta[0:1], fibres // 2, 1), meta[1:2])
            chosen = (iota((slots, fibres), 0) == slot).astype(BF16)
            both = jnp.concatenate(split(values), 1)
            sorted_ = jnp.dot(chosen, both, preferred_element_type=F32).astype(BF16)
            for s in range(sectors):
                placed[s, d * capacity : (d + 1) * capacity, :] = sorted_[s * capacity : (s + 1) * capacity]
            at = (d % per) * capacity
            inside = (lane8 >= at) & (lane8 < at + capacity)
            for g in range(sectors // 8):
                moved = pltpu.roll(meta, (at - g * capacity) % slab, 1)
                code_parts[g][d // per] = jnp.where(inside, moved, code_parts[g][d // per])
        codes = [jnp.concatenate(parts, 1) for parts in code_parts]
        for s in range(sectors):
            code = codes[s // 8][s % 8 : s % 8 + 1]
            within = jnp.floor(code * (1.0 / radii))
            radius = code - radii * within
            at_radius = (iota((radii, depth), 0) == radius).astype(BF16)
            rows = jnp.dot(basis_pair, at_radius, preferred_element_type=F32).astype(BF16)
            mask = (iota((sector_width, depth), 0) + 1.0 == within).astype(BF16)
            weights = (rows[:, None, :] * mask[None]).reshape(2 * own * sector_width, depth)
            product = jnp.dot(weights, placed[s], preferred_element_type=F32)
            size = own * sector_width
            total = product[:size, :slab] + product[:size, slab:] + product[size:, :slab]
            for j in range(own):
                for e in range(2):
                    first = j * sector_width + e * half
                    columns[j, e, s * half : (s + 1) * half, :] = total[first : first + half]

    parts = []
    quarter = table_high.shape[2] // 2
    for e in range(2):
        turned = [jnp.transpose(columns[step * group + i, e]) for i in range(group)]
        high, low = split(jnp.concatenate(turned, 0))
        parts.append(
            jnp.dot(high, table_high[e], preferred_element_type=F32)
            + jnp.dot(low, table_high[e], preferred_element_type=F32)
            + jnp.dot(high, table_low[e], preferred_element_type=F32)
        )
    total, difference = parts[0] + parts[1], parts[0] - parts[1]
    tiles = quarter // 128
    for i in range(group):
        for c in range(2):
            for t in range(2 * tiles):
                source = total if t < tiles else difference
                lanes = c * quarter + (t % tiles) * 128
                scale = scales[step * group + i, :1, t * 128 : (t + 1) * 128]
                value = source[i * slab : (i + 1) * slab, lanes : lanes + 128] * scale
                line = (4 * tiles) * slab * i + 2 * t + c
                out_ref[pl.ds(line, slab, stride=4 * tiles), :] = value


def dft_tables():
    half = AZ // 2
    wave, place = np.meshgrid(np.arange(half), np.arange(half))
    tables = []
    for e in range(2):
        phase = (wave * (2 * place + e) % AZ) * (2.0 * np.pi / AZ)
        tables.append(np.concatenate([np.cos(phase), -np.sin(phase)], 1) / np.sqrt(AZ))
    exact = np.stack(tables).astype(np.float32)
    high = jnp.asarray(exact).astype(BF16)
    low = (jnp.asarray(exact) - high.astype(F32)).astype(BF16)
    return high, low


def gather(pieces):
    sectors = lax.axis_size("sec")

    def swap(value, bits):
        return lax.ppermute(value, "sec", [(i, i ^ bits) for i in range(sectors)])

    other = lax.ppermute(pieces[1], "rad", [(0, 1), (1, 0)])
    held = []
    for value in (pieces[0], other):
        along = [value] + [swap(value, bits) for bits in range(4, sectors, 4)]
        across = along + [swap(v, 2) for v in along]
        held += across + [swap(v, 1) for v in across]
    return held


def per_device(
    transmembrane_potential,
    channel_openness,
    longitudinal_conductance,
    sector_map,
    cell_index,
    innervating_neuron,
    activation_moment,
    synapse_position,
    radial_basis_matrix,
    spectrum,
):
    fibres, points = transmembrane_potential.shape
    sectors, bands = lax.axis_size("sec"), lax.axis_size("rad")
    slab = points // bands
    sector_width = AZ // sectors
    own = spectrum.shape[0]
    vmem = pl.BlockSpec(memory_space=pltpu.VMEM)
    smem = pl.BlockSpec(memory_space=pltpu.SMEM)
    band = lax.axis_index("rad").astype(jnp.int32).reshape(1)
    volt, gates, pieces = pl.pallas_call(
        functools.partial(
            fibre_kernel,
            sectors=sectors,
            sector_width=sector_width,
            band_rows=RAD // bands,
            chunk=16,
        ),
        out_shape=(
            jax.ShapeDtypeStruct((fibres, points), F32),
            jax.ShapeDtypeStruct((3, fibres, points), F32),
            jax.ShapeDtypeStruct((bands, fibres + 8, slab), F32),
        ),
        in_specs=[smem] + [vmem] * 8,
        out_specs=(vmem, vmem, vmem),
        scratch_shapes=[pltpu.VMEM((fibres, points), F32), pltpu.VMEM((fibres, points), F32)],
    )(
        band,
        transmembrane_potential,
        channel_openness,
        longitudinal_conductance.reshape(1, fibres),
        sector_map.reshape(1, fibres),
        cell_index.reshape(1, fibres),
        innervating_neuron.reshape(1, fibres),
        activation_moment.reshape(1, -1),
        synapse_position.reshape(1, fibres),
    )
    held = gather(pieces)
    count = len(held)
    capacity = 2 * fibres // sectors
    group = 4
    high, low = dft_tables()
    start = (lax.axis_index("sec") * own).astype(jnp.int32).reshape(1)
    lines = own * slab * 2 * AZ // 128

    def whole(array):
        rank = len(array.shape)
        return pl.BlockSpec(array.shape, lambda g: (0,) * rank, pipeline_mode=pl.Buffered(1))

    flat = pl.pallas_call(
        functools.partial(
            grid_kernel, count=count, sectors=sectors, sector_width=sector_width, group=group
        ),
        out_shape=jax.ShapeDtypeStruct((lines, 128), F32),
        grid=(own // group,),
        in_specs=[smem]
        + [whole(v) for v in held]
        + [whole(v) for v in (radial_basis_matrix, high, low, spectrum)],
        out_specs=pl.BlockSpec((lines * group // own, 128), lambda g: (g, 0)),
        scratch_shapes=[
            pltpu.VMEM((sectors, count * capacity, 2 * slab), BF16),
            pltpu.VMEM((own, 2, AZ // 2, slab), F32),
            pltpu.VMEM((RAD, RAD), F32),
            pltpu.VMEM((own, 8, AZ), F32),
        ],
    )(start, *held, radial_basis_matrix, high, low, spectrum)
    tiled = flat.reshape(own, slab, AZ // 128, 2, 128)
    potential = tiled.transpose(0, 1, 3, 2, 4).reshape(own, slab, 2, AZ)
    return volt, gates, potential


def solution(mesh):
    placed = (
        P(("sec", "rad"), None),
        P(None, ("sec", "rad"), None),
        P(("sec", "rad")),
        P(("sec", "rad"), None),
        P(("sec", "rad")),
        P(("sec", "rad")),
        P(),
        P(("sec", "rad")),
        P(),
        P("sec", None),
    )
    fits = mesh.shape["rad"] == 2 and mesh.shape["sec"] == 16
    return jax.shard_map(
        per_device if fits else per_device_general,
        mesh=mesh,
        in_specs=placed,
        out_specs=(
            P(("sec", "rad"), None),
            P(None, ("sec", "rad"), None),
            P("sec", "rad", None, None),
        ),
        check_vma=False,
    )
```
